1024 devices in a mesh: seq: 64 (over x, y_lo, core), chan: 16 (over y_hi, z).
Axes of the slice: x: 8, y: 8 (y_hi: 2, y_lo: 4; y = y_hi * 4 + y_lo), z: 8, core: 2. Of those that a mesh axis runs over, the one named last changes fastest.
Arguments:
- features: bfloat16 [16384, 3, 8192], P(('seq', 'chan')), may hold values from -6 to 6
- short_taps: float32 [7, 3, 8192], P(None, None, 'chan'), may hold values from -2 to 2
- mr_filter: float32 [512, 128], P('chan'), may hold values from -0.5 to 0.5
- out_weight: bfloat16 [8192, 4096], P('chan', 'seq'), may hold values from -0.1875 to 0.1875
- residual: bfloat16 [16384, 4096], P('seq', 'chan'), may hold values from -6 to 6
Outputs:
- block_out: bfloat16 [16384, 4096], P('seq', 'chan')
The draws below stay inside these ranges and needn't reach their ends.
All inputs are finite; a program needn't handle non-finite values.
Results may differ from the reference program's by a relative error of at most 0.015.
Values may be sent and summed in bfloat16 or wider, within the bound.
No kernel may reach another device: no remote copies, remote signals or barrier semaphores. Data moves between devices by JAX's collectives and lax.ppermute only.
A program may use at most 64 MiB of HBM per device.

```python
import jax
import jax.numpy as jnp
from jax import lax

D = 8192
GROUPS = 512
D_OUT = 4096
KS = 7
KMR = 128
TOKENS = 16384
N_CHAN = 16


def raised(values, rng, source, target, parts, factor):
    owner, partner = [(jnp.arange(values.shape[dim]) // (values.shape[dim] // parts)).reshape([-1 if axis == dim else 1 for axis in range(values.ndim)]) for dim in (source, target)]
    chosen = jax.random.permutation(rng, parts)[partner]
    strong = (owner == chosen) | (owner == (partner + parts // 2) % parts)
    return jnp.where(strong, factor * values, values)


def shard_levels(key, extent, shards, smallest, high):
    factor_of, own = 1.0, jax.random.fold_in(key, 6)
    for axis_at, blocks in shards:
        steps = jnp.exp(jax.random.uniform(jax.random.fold_in(own, axis_at), (blocks,), jnp.float32, smallest / len(shards), high / len(shards)))
        factor_of = factor_of * jnp.repeat(steps, extent[axis_at] // blocks).reshape([-1 if axis == axis_at else 1 for axis in range(len(extent))])
    return factor_of


def normal_values(rng, extent, width, most, shards=(), kind=jnp.bfloat16):
    array = width * jax.random.normal(rng, extent, jnp.float32)
    if shards:
        array = array * shard_levels(rng, extent, shards, -0.22, 0.18)
    return jnp.clip(array, -most, most).astype(kind)


def heavy_noise(stream_key, dims, scale, reach, pieces, heavy, kind=jnp.bfloat16):
    values = scale * jax.random.normal(stream_key, dims, jnp.float32)
    if pieces:
        values = values * shard_levels(stream_key, dims, pieces, -0.22, 0.18)
    return jnp.clip(raised(values, jax.random.fold_in(stream_key, 3), *heavy), -reach, reach).astype(kind)


def setup_inputs(seed: int = 0) -> dict:
    arg_keys = jax.random.split(jax.random.key(seed), 6)
    return {
        "features": normal_values(arg_keys[0], (TOKENS, 3, D), 1.0, 6.0, ((0, 1024),)),
        "short_taps": normal_values(arg_keys[1], (KS, 3, D), KS ** -0.5, 2.0, ((2, 16),), jnp.float32),
        "mr_filter": normal_values(arg_keys[2], (GROUPS, KMR), KMR ** -0.5, 0.5, ((0, 16),), jnp.float32),
        "out_weight": heavy_noise(arg_keys[3], (D, D_OUT), D ** -0.5, 0.1875, ((0, 16), (1, 64)), (0, 1, 64, 4.0)),
        "residual": normal_values(arg_keys[4], (TOKENS, D_OUT), 1.0, 6.0, ((0, 64), (1, 16))),
    }


def short_filter(padded, tap_table, out_count):
    widened = padded.astype(jnp.float32)
    result = jnp.zeros((out_count,) + widened.shape[1:], jnp.float32)
    for offset in range(KS):
        first_row = KS - 1 - offset
        result = result + tap_table[offset] * widened[first_row:first_row + out_count]
    return result


def band_tables(filters):
    tap_span = filters.shape[1]
    later_pos = jnp.arange(tap_span, dtype=jnp.int32)[:, None, None]
    earlier_pos = jnp.arange(tap_span, dtype=jnp.int32)[None, :, None]
    lag_pos = jnp.arange(tap_span, dtype=jnp.int32)[None, None, :]
    near_pick = (lag_pos == later_pos - earlier_pos).astype(jnp.float32)
    far_pick = (lag_pos == later_pos - earlier_pos + tap_span).astype(jnp.float32)
    near_band = jnp.einsum('tsj,gj->gts', near_pick, filters, precision=lax.Precision.HIGHEST)
    far_band = jnp.einsum('tsj,gj->gts', far_pick, filters, precision=lax.Precision.HIGHEST)
    return near_band, far_band


def medium_conv(extended, filters):
    total_rows, chan_count = extended.shape
    groups = filters.shape[0]
    group_size = chan_count // groups
    blocks = extended.reshape(total_rows // KMR, KMR, groups, group_size)
    near_band, far_band = band_tables(filters)
    result = jnp.einsum('gts,nsgc->ntgc', near_band, blocks[1:], precision=lax.Precision.HIGHEST)
    result = result + jnp.einsum('gts,nsgc->ntgc', far_band, blocks[:-1], precision=lax.Precision.HIGHEST)
    return result.reshape(-1, chan_count)


def reference(features, short_taps, mr_filter, out_weight, residual):
    chan_count = D // N_CHAN
    group_count = GROUPS // N_CHAN
    row_count = features.shape[0]

    def accumulate(running, block_index):
        first_chan = (block_index * chan_count).astype(jnp.int32)
        first_group = (block_index * group_count).astype(jnp.int32)
        chan_block = lax.dynamic_slice_in_dim(features, first_chan, chan_count, 2)
        tap_table = lax.dynamic_slice_in_dim(short_taps, first_chan, chan_count, 2)
        filters = lax.dynamic_slice_in_dim(mr_filter, first_group, group_count, 0)
        weight = lax.dynamic_slice_in_dim(out_weight, first_chan, chan_count, 0)
        padded = jnp.concatenate([jnp.zeros((KS - 1, 3, chan_count), chan_block.dtype), chan_block], axis=0)
        short_out = short_filter(padded, tap_table, row_count)
        inner_term = short_out[:, 1, :] * short_out[:, 2, :]
        extended = jnp.concatenate([jnp.zeros((KMR, chan_count), jnp.float32), inner_term], axis=0)
        mixed_out = medium_conv(extended, filters)
        gated_out = (short_out[:, 0, :] * mixed_out).astype(jnp.bfloat16)
        partial_value = jnp.dot(gated_out, weight, preferred_element_type=jnp.float32).astype(jnp.bfloat16)
        partial_value = lax.optimization_barrier(partial_value)
        return running + partial_value.astype(jnp.float32), None

    start_sum = jnp.zeros((row_count, out_weight.shape[1]), jnp.float32)
    summed, _ = lax.scan(accumulate, start_sum, jnp.arange(N_CHAN, dtype=jnp.int32))
    return (residual.astype(jnp.float32) + summed).astype(jnp.bfloat16)
```

```python
import jax
import jax.numpy as jnp
from jax import lax
from jax.experimental import pallas as pl
from jax.experimental.pallas import tpu as pltpu
from jax.sharding import Mesh
from jax.sharding import PartitionSpec as P

KS = 7
KMR = 128
GROUP = 16
LANES = 128
INTERPRET = False

SEQ = ("x", "yh", "yl", "core")
CHAN = ("Y", "zz", "par")


def call(kernel, flops=0, moved=0, vmem_mib=16, **kwargs):
    cost = pl.CostEstimate(flops=flops, bytes_accessed=moved, transcendentals=0)
    params = pltpu.CompilerParams(vmem_limit_bytes=vmem_mib << 20)
    return pl.pallas_call(
        kernel, interpret=INTERPRET, cost_estimate=cost, compiler_params=params, **kwargs
    )


def bands_kernel(filter_ref, band_ref):
    row = lax.broadcasted_iota(jnp.int32, (KMR, KMR), 0)
    lane = lax.broadcasted_iota(jnp.int32, (KMR, KMR), 1)
    for group in range(filter_ref.shape[0]):
        taps = jnp.broadcast_to(filter_ref[group : group + 1, :], (KMR, KMR))
        rolled = pltpu.roll(taps, 0, 1, stride=1, stride_axis=0)
        band_ref[group, :KMR, :] = jnp.where(lane < row, rolled, 0.0).astype(band_ref.dtype)
        band_ref[group, KMR:, :] = jnp.where(lane >= row, rolled, 0.0).astype(band_ref.dtype)


def short_rows(ext_ref, taps, first, count):
    total = taps[0:1] * ext_ref[first : first + count, :]
    for offset in range(1, KS):
        total = total + taps[offset : offset + 1] * ext_ref[first - offset : first - offset + count, :]
    return total


def conv_kernel(rows_ref, halo_ref, taps_ref, band_ref, gated_ref, q_ext, k_ext, v_ext, inner_t, mixed_t):
    sources, _, block, _ = rows_ref.shape
    tokens = sources * block
    halo_blocks = (halo_ref.shape[0] - 1) // 2
    halo = halo_blocks * block
    q_ext[:block, :] = halo_ref[2 * halo_blocks].astype(jnp.float32)
    for i in range(halo_blocks):
        k_ext[i * block : (i + 1) * block, :] = halo_ref[2 * i].astype(jnp.float32)
        v_ext[i * block : (i + 1) * block, :] = halo_ref[2 * i + 1].astype(jnp.float32)
    for i in range(sources):
        q_ext[block + i * block : block + (i + 1) * block, :] = rows_ref[i, 0].astype(jnp.float32)
        k_ext[halo + i * block : halo + (i + 1) * block, :] = rows_ref[i, 1].astype(jnp.float32)
        v_ext[halo + i * block : halo + (i + 1) * block, :] = rows_ref[i, 2].astype(jnp.float32)
    taps_q, taps_k, taps_v = (taps_ref[i] for i in range(3))
    for i in range(tokens // KMR + 1):
        first = halo - KMR + i * KMR
        inner = short_rows(k_ext, taps_k, first, KMR) * short_rows(v_ext, taps_v, first, KMR)
        inner_t[:, i * KMR : (i + 1) * KMR] = inner.T.astype(inner_t.dtype)
    spans = tokens // KMR
    for group in range(band_ref.shape[0]):
        chans = slice(group * GROUP, (group + 1) * GROUP)
        pieces = [inner_t[chans, i * KMR : (i + 2) * KMR] for i in range(spans)]
        out = jnp.dot(
            jnp.concatenate(pieces, axis=0), band_ref[group], preferred_element_type=jnp.float32
        )
        for i in range(spans):
            mixed_t[chans, i * KMR : (i + 1) * KMR] = out[i * GROUP : (i + 1) * GROUP]
    for i in range(spans):
        query = short_rows(q_ext, taps_q, block + i * KMR, KMR)
        mixed = mixed_t[:, i * KMR : (i + 1) * KMR].T
        gated_ref[i * KMR : (i + 1) * KMR, :] = (query * mixed).astype(gated_ref.dtype)


def project_kernel(par_ref, own_ref, pair_ref, mine_ref, other_ref, out_ref, both):
    @pl.when(pl.program_id(0) == 0)
    def _():
        par = par_ref[0]
        both[par] = own_ref[...]
        both[1 - par] = pair_ref[...]

    total = None
    for b in range(2):
        pieces = []
        for yl in range(mine_ref.shape[2]):
            pieces += [mine_ref[0, b, yl], other_ref[0, b, yl]]
        term = lax.dot_general(
            both[b],
            jnp.concatenate(pieces, axis=0),
            (((1,), (1,)), ((), ())),
            preferred_element_type=jnp.float32,
        )
        total = term if total is None else total + term
    out_ref[0] = total.astype(out_ref.dtype)


def sum_kernel(core_ref, parts_ref, residual_ref, out_ref):
    total = parts_ref[0].astype(jnp.float32)
    for i in range(1, parts_ref.shape[0]):
        total = total + parts_ref[i].astype(jnp.float32)
    for i in range(total.shape[1] // LANES):
        lanes = slice(i * LANES, (i + 1) * LANES)
        piece = total[:, lanes]
        piece = jnp.where(core_ref[0] == 0, piece, pltpu.roll(piece, LANES // 2, 1))
        out_ref[:, lanes] = (residual_ref[:, lanes].astype(jnp.float32) + piece).astype(out_ref.dtype)


def body(features, short_taps, mr_filter, out_weight, residual):
    block, _, width = features.shape
    sources = lax.axis_size(CHAN)
    chans = width // sources
    tokens = sources * block
    bf16, f32 = jnp.bfloat16, jnp.float32
    vmem = pl.BlockSpec(memory_space=pltpu.VMEM)
    smem = pl.BlockSpec(memory_space=pltpu.SMEM)

    weight = lax.ppermute(out_weight.T, ("yh", "par"), [(0, 0), (1, 2), (2, 1), (3, 3)])
    cols = weight.shape[0]
    near = lax.all_gather(weight, ("yh", "yl"), axis=0)
    mine = lax.all_gather(near, "x", axis=0)
    x_size = mine.shape[0]
    yl_size = lax.axis_size("yl")
    mine = mine.reshape(x_size, 2, yl_size, cols, chans)

    sent = features.reshape(block, 3, sources, chans).transpose(2, 1, 0, 3)
    rows = lax.all_to_all(sent, CHAN, 0, 0, tiled=True)
    halo_blocks = -(-(KMR + KS - 1) // block)
    tail = jnp.concatenate(
        [rows[sources - halo_blocks :, 1:].reshape(2 * halo_blocks, block, chans), rows[sources - 1 :, 0]],
        axis=0,
    )
    shards = lax.axis_size(SEQ)
    halo = lax.ppermute(tail, SEQ, [(i, i + 1) for i in range(shards - 1)])

    groups = mr_filter.shape[0]
    band = call(
        bands_kernel,
        flops=groups * KMR * KMR * 4,
        moved=groups * 2 * KMR * KMR * 2,
        out_shape=jax.ShapeDtypeStruct((groups, 2 * KMR, KMR), bf16),
        in_specs=[vmem],
        out_specs=vmem,
    )(mr_filter)

    per_step = LANES // GROUP
    halo_rows = halo_blocks * block
    gated = call(
        conv_kernel,
        flops=tokens * chans * 256 * 2,
        moved=rows.size * 2 + halo.size * 2 + band.size * 2,
        grid=(chans // LANES,),
        out_shape=jax.ShapeDtypeStruct((tokens, chans), bf16),
        in_specs=[
            pl.BlockSpec((sources, 3, block, LANES), lambda i: (0, 0, 0, i)),
            pl.BlockSpec((2 * halo_blocks + 1, block, LANES), lambda i: (0, 0, i)),
            pl.BlockSpec((3, KS, LANES), lambda i: (0, 0, i)),
            pl.BlockSpec((per_step, 2 * KMR, KMR), lambda i: (i, 0, 0)),
        ],
        out_specs=pl.BlockSpec((tokens, LANES), lambda i: (0, i)),
        scratch_shapes=[
            pltpu.VMEM((block + tokens, LANES), f32),
            pltpu.VMEM((halo_rows + tokens, LANES), f32),
            pltpu.VMEM((halo_rows + tokens, LANES), f32),
            pltpu.VMEM((LANES, KMR + tokens), bf16),
            pltpu.VMEM((LANES, tokens), f32),
        ],
    )(rows, halo, short_taps.transpose(1, 0, 2), band)

    pair = lax.ppermute(gated, "par", [(0, 1), (1, 0)])
    mine, gated = lax.optimization_barrier((mine, gated))
    other = lax.ppermute(mine, "core", [(0, 1), (1, 0)])
    out_cols = 2 * yl_size * cols
    whole = pl.BlockSpec((tokens, chans), lambda i: (0, 0))
    slab = pl.BlockSpec((1, 2, yl_size, cols, chans), lambda i: (i, 0, 0, 0, 0))
    partial = call(
        project_kernel,
        flops=tokens * 2 * chans * x_size * out_cols * 2,
        moved=mine.size * 4 + x_size * tokens * out_cols * 2 + gated.size * 4,
        grid=(x_size,),
        out_shape=jax.ShapeDtypeStruct((x_size, tokens, out_cols), bf16),
        in_specs=[smem, whole, whole, slab, slab],
        out_specs=pl.BlockSpec((1, tokens, out_cols), lambda i: (i, 0, 0)),
        scratch_shapes=[pltpu.VMEM((2, tokens, chans), bf16)],
    )(lax.axis_index("par").reshape(1), gated, pair, mine, other)

    parts = lax.all_to_all(partial, ("Y", "zz"), 0, 0, tiled=True)
    return call(
        sum_kernel,
        flops=parts.size,
        moved=parts.size * 2 + residual.size * 4,
        out_shape=jax.ShapeDtypeStruct(residual.shape, residual.dtype),
        in_specs=[smem, vmem, vmem],
        out_specs=vmem,
    )(lax.axis_index("core").reshape(1), parts, residual)


def split(mesh, sizes):
    return Mesh(mesh.devices.reshape(sizes), SEQ + CHAN)


def solution(mesh):
    fine = split(mesh, (8, 2, 2, 2, 2, 4, 2))
    placed = (
        P(SEQ + CHAN, None, None),
        P(None, None, CHAN),
        P(CHAN, None),
        P(CHAN, SEQ),
        P(SEQ, CHAN),
    )
    return jax.shard_map(body, mesh=fine, in_specs=placed, out_specs=P(SEQ, CHAN), check_vma=False)
```

```python
import jax
import jax.numpy as jnp
from jax import lax
from jax.experimental import pallas as pl
from jax.experimental.pallas import tpu as pltpu
from jax.sharding import Mesh
from jax.sharding import PartitionSpec as P


KS = 7
KMR = 128
GROUP = 16
LANES = 128
INTERPRET = False

SEQ = ("x", "yh", "yl", "core")
CHAN = ("Y", "zz", "par")


def call(kernel, flops=0, moved=0, vmem_mib=16, **kwargs):
    cost = pl.CostEstimate(flops=flops, bytes_accessed=moved, transcendentals=0)
    params = pltpu.CompilerParams(vmem_limit_bytes=vmem_mib << 20)
    return pl.pallas_call(
        kernel, interpret=INTERPRET, cost_estimate=cost, compiler_params=params, **kwargs
    )


def bands_kernel(filter_ref, band_ref):
    row = lax.broadcasted_iota(jnp.int32, (KMR, KMR), 0)
    lane = lax.broadcasted_iota(jnp.int32, (KMR, KMR), 1)
    for group in range(filter_ref.shape[0]):
        taps = jnp.broadcast_to(filter_ref[group : group + 1, :], (KMR, KMR))
        rolled = pltpu.roll(taps, 0, 1, stride=1, stride_axis=0)
        band_ref[group, :KMR, :] = jnp.where(lane < row, rolled, 0.0).astype(band_ref.dtype)
        band_ref[group, KMR:, :] = jnp.where(lane >= row, rolled, 0.0).astype(band_ref.dtype)


def short_rows(ext_ref, taps, first, count):
    total = taps[0:1] * ext_ref[first : first + count, :]
    for offset in range(1, KS):
        total = total + taps[offset : offset + 1] * ext_ref[first - offset : first - offset + count, :]
    return total


def conv_kernel(rows_ref, halo_ref, taps_ref, band_ref, gated_ref, q_ext, k_ext, v_ext, inner_t, mixed_t):
    sources, _, block, _ = rows_ref.shape
    tokens = sources * block
    halo_blocks = (halo_ref.shape[0] - 1) // 2
    halo = halo_blocks * block
    q_ext[:block, :] = halo_ref[2 * halo_blocks].astype(jnp.float32)
    for i in range(halo_blocks):
        k_ext[i * block : (i + 1) * block, :] = halo_ref[2 * i].astype(jnp.float32)
        v_ext[i * block : (i + 1) * block, :] = halo_ref[2 * i + 1].astype(jnp.float32)
    for i in range(sources):
        q_ext[block + i * block : block + (i + 1) * block, :] = rows_ref[i, 0].astype(jnp.float32)
        k_ext[halo + i * block : halo + (i + 1) * block, :] = rows_ref[i, 1].astype(jnp.float32)
        v_ext[halo + i * block : halo + (i + 1) * block, :] = rows_ref[i, 2].astype(jnp.float32)
    taps_q, taps_k, taps_v = (taps_ref[i] for i in range(3))
    for i in range(tokens // KMR + 1):
        first = halo - KMR + i * KMR
        inner = short_rows(k_ext, taps_k, first, KMR) * short_rows(v_ext, taps_v, first, KMR)
        inner_t[:, i * KMR : (i + 1) * KMR] = inner.T.astype(inner_t.dtype)
    spans = tokens // KMR
    for group in range(band_ref.shape[0]):
        chans = slice(group * GROUP, (group + 1) * GROUP)
        pieces = [inner_t[chans, i * KMR : (i + 2) * KMR] for i in range(spans)]
        out = jnp.dot(
            jnp.concatenate(pieces, axis=0), band_ref[group], preferred_element_type=jnp.float32
        )
        for i in range(spans):
            mixed_t[chans, i * KMR : (i + 1) * KMR] = out[i * GROUP : (i + 1) * GROUP]
    for i in range(spans):
        query = short_rows(q_ext, taps_q, block + i * KMR, KMR).T
        mixed = mixed_t[:, i * KMR : (i + 1) * KMR]
        gated_ref[:, i * KMR : (i + 1) * KMR] = (query * mixed).astype(gated_ref.dtype)


def project_kernel(place_ref, own_ref, pair_ref, weight_ref, out_ref, both):
    @pl.when(pl.program_id(0) == 0)
    def _():
        slot = place_ref[0]
        both[slot] = own_ref[...]
        both[1 - slot] = pair_ref[...]

    steps, cores, _, yl_size, _, _ = weight_ref.shape
    for step in range(steps):
        total = None
        for slot in range(2):
            pieces = [weight_ref[step, core, slot, yl] for yl in range(yl_size) for core in range(cores)]
            term = jnp.dot(
                jnp.concatenate(pieces, axis=0), both[slot], preferred_element_type=jnp.float32
            )
            total = term if total is None else total + term
        out_ref[step] = total.astype(out_ref.dtype)


def sum_kernel(place_ref, parts_ref, residual_ref, out_ref):
    total = parts_ref[0].astype(jnp.float32)
    for i in range(1, parts_ref.shape[0]):
        total = total + parts_ref[i].astype(jnp.float32)
    half = total.shape[0] // 2
    first, second = total[:half], total[half:]
    for i, (piece, swapped) in enumerate(((first, second), (second, first))):
        lanes = slice(i * half, (i + 1) * half)
        piece = jnp.where(place_ref[0] == 0, piece, swapped).T
        out_ref[:, lanes] = (residual_ref[:, lanes].astype(jnp.float32) + piece).astype(out_ref.dtype)


def weight_route(pair_step, yl_step):
    return [
        ((yh * 2 + yl) * 2 + par, ((par ^ pair_step) * 2 + (yl ^ yl_step)) * 2 + yh)
        for yh in range(2)
        for yl in range(2)
        for par in range(2)
    ]


def body(features, short_taps, mr_filter, out_weight, residual):
    block, _, width = features.shape
    sources = lax.axis_size(CHAN)
    chans = width // sources
    tokens = sources * block
    bf16, f32 = jnp.bfloat16, jnp.float32
    vmem = pl.BlockSpec(memory_space=pltpu.VMEM)
    smem = pl.BlockSpec(memory_space=pltpu.SMEM)

    near = [
        lax.ppermute(out_weight.T, ("yh", "yl", "par"), weight_route(pair_step, yl_step))
        for pair_step in range(2)
        for yl_step in range(2)
    ]
    cols = near[0].shape[0]
    near = jnp.stack(near).reshape(2, 2, cols, chans)
    whole_weight = lax.all_gather(near, ("x", "core"), axis=0)
    x_size = lax.axis_size("x")
    whole_weight = whole_weight.reshape(x_size, -1, *near.shape)

    sent = features.reshape(block, 3, sources, chans).transpose(2, 1, 0, 3)
    rows = lax.all_to_all(sent, CHAN, 0, 0, tiled=True)
    halo_blocks = -(-(KMR + KS - 1) // block)
    tail = jnp.concatenate(
        [rows[sources - halo_blocks :, 1:].reshape(2 * halo_blocks, block, chans), rows[sources - 1 :, 0]],
        axis=0,
    )
    shards = lax.axis_size(SEQ)
    halo = lax.ppermute(tail, SEQ, [(i, i + 1) for i in range(shards - 1)])

    groups = mr_filter.shape[0]
    band = call(
        bands_kernel,
        flops=groups * KMR * KMR * 4,
        moved=groups * 2 * KMR * KMR * 2,
        out_shape=jax.ShapeDtypeStruct((groups, 2 * KMR, KMR), bf16),
        in_specs=[vmem],
        out_specs=vmem,
    )(mr_filter)

    per_step = LANES // GROUP
    halo_rows = halo_blocks * block
    gated = call(
        conv_kernel,
        flops=tokens * chans * 256 * 2,
        moved=rows.size * 2 + halo.size * 2 + band.size * 2,
        grid=(chans // LANES,),
        out_shape=jax.ShapeDtypeStruct((chans, tokens), bf16),
        in_specs=[
            pl.BlockSpec((sources, 3, block, LANES), lambda i: (0, 0, 0, i)),
            pl.BlockSpec((2 * halo_blocks + 1, block, LANES), lambda i: (0, 0, i)),
            pl.BlockSpec((3, KS, LANES), lambda i: (0, 0, i)),
            pl.BlockSpec((per_step, 2 * KMR, KMR), lambda i: (i, 0, 0)),
        ],
        out_specs=pl.BlockSpec((LANES, tokens), lambda i: (i, 0)),
        scratch_shapes=[
            pltpu.VMEM((block + tokens, LANES), f32),
            pltpu.VMEM((halo_rows + tokens, LANES), f32),
            pltpu.VMEM((halo_rows + tokens, LANES), f32),
            pltpu.VMEM((LANES, KMR + tokens), bf16),
            pltpu.VMEM((LANES, tokens), f32),
        ],
    )(rows, halo, short_taps.transpose(1, 0, 2), band)

    pair = lax.ppermute(gated, "par", [(0, 1), (1, 0)])
    whole_weight, pair = lax.optimization_barrier((whole_weight, pair))
    out_cols = whole_weight.size // (x_size * 2 * chans)
    both = pl.BlockSpec((chans, tokens), lambda i: (0, 0))
    per_call = 2
    partial = call(
        project_kernel,
        vmem_mib=20,
        flops=tokens * 2 * chans * x_size * out_cols * 2,
        moved=whole_weight.size * 2 + x_size * tokens * out_cols * 2 + gated.size * 4,
        grid=(x_size // per_call,),
        out_shape=jax.ShapeDtypeStruct((x_size, out_cols, tokens), bf16),
        in_specs=[
            smem,
            both,
            both,
            pl.BlockSpec((per_call, *whole_weight.shape[1:]), lambda i: (i, 0, 0, 0, 0, 0)),
        ],
        out_specs=pl.BlockSpec((per_call, out_cols, tokens), lambda i: (i, 0, 0)),
        scratch_shapes=[pltpu.VMEM((2, chans, tokens), bf16)],
    )((lax.axis_index("par") ^ lax.axis_index("yh")).reshape(1), gated, pair, whole_weight)

    parts = lax.all_to_all(partial, ("Y", "zz"), 0, 0, tiled=True)
    return call(
        sum_kernel,
        flops=parts.size,
        moved=parts.size * 2 + residual.size * 4,
        out_shape=jax.ShapeDtypeStruct(residual.shape, residual.dtype),
        in_specs=[smem, vmem, vmem],
        out_specs=vmem,
    )(lax.axis_index("yl").reshape(1), parts, residual)


def split(mesh, sizes):
    return Mesh(mesh.devices.reshape(sizes), SEQ + CHAN)


def solution(mesh):
    fine = split(mesh, (8, 2, 2, 2, 2, 4, 2))
    placed = (
        P(SEQ + CHAN, None, None),
        P(None, None, CHAN),
        P(CHAN, None),
        P(CHAN, SEQ),
        P(SEQ, CHAN),
    )
    return jax.shard_map(body, mesh=fine, in_specs=placed, out_specs=P(SEQ, CHAN), check_vma=False)
```

```python
import jax
import jax.numpy as jnp
from jax import lax
from jax.experimental import pallas as pl
from jax.experimental.pallas import tpu as pltpu
from jax.sharding import Mesh
from jax.sharding import PartitionSpec as P


KS = 7
KMR = 128
GROUP = 16
LANES = 128
INTERPRET = False

SEQ = ("x", "yh", "yl", "core")
CHAN = ("Y", "zz", "par")


def call(kernel, flops=0, moved=0, vmem_mib=16, **kwargs):
    cost = pl.CostEstimate(flops=flops, bytes_accessed=moved, transcendentals=0)
    params = pltpu.CompilerParams(vmem_limit_bytes=vmem_mib << 20)
    return pl.pallas_call(
        kernel, interpret=INTERPRET, cost_estimate=cost, compiler_params=params, **kwargs
    )


def bands_kernel(filter_ref, band_ref):
    row = lax.broadcasted_iota(jnp.int32, (KMR, KMR), 0)
    lane = lax.broadcasted_iota(jnp.int32, (KMR, KMR), 1)
    for group in range(filter_ref.shape[0]):
        taps = jnp.broadcast_to(filter_ref[group : group + 1, :], (KMR, KMR))
        rolled = pltpu.roll(taps, 0, 1, stride=1, stride_axis=0)
        band_ref[group, :KMR, :] = jnp.where(lane < row, rolled, 0.0).astype(band_ref.dtype)
        band_ref[group, KMR:, :] = jnp.where(lane >= row, rolled, 0.0).astype(band_ref.dtype)


def short_rows(ext_ref, taps, first, count):
    total = taps[0:1] * ext_ref[first : first + count, :]
    for offset in range(1, KS):
        total = total + taps[offset : offset + 1] * ext_ref[first - offset : first - offset + count, :]
    return total


def conv_kernel(rows_ref, halo_ref, taps_ref, band_ref, gated_ref, q_ext, k_ext, v_ext, inner_t, mixed_t):
    sources, _, block, _ = rows_ref.shape
    tokens = sources * block
    halo_blocks = (halo_ref.shape[0] - 1) // 2
    halo = halo_blocks * block
    q_ext[:block, :] = halo_ref[2 * halo_blocks].astype(jnp.float32)
    for i in range(halo_blocks):
        k_ext[i * block : (i + 1) * block, :] = halo_ref[2 * i].astype(jnp.float32)
        v_ext[i * block : (i + 1) * block, :] = halo_ref[2 * i + 1].astype(jnp.float32)
    for i in range(sources):
        q_ext[block + i * block : block + (i + 1) * block, :] = rows_ref[i, 0].astype(jnp.float32)
        k_ext[halo + i * block : halo + (i + 1) * block, :] = rows_ref[i, 1].astype(jnp.float32)
        v_ext[halo + i * block : halo + (i + 1) * block, :] = rows_ref[i, 2].astype(jnp.float32)
    taps_q, taps_k, taps_v = (taps_ref[i] for i in range(3))
    for i in range(tokens // KMR + 1):
        first = halo - KMR + i * KMR
        inner = short_rows(k_ext, taps_k, first, KMR) * short_rows(v_ext, taps_v, first, KMR)
        inner_t[:, i * KMR : (i + 1) * KMR] = inner.T.astype(inner_t.dtype)
    spans = tokens // KMR
    for group in range(band_ref.shape[0]):
        chans = slice(group * GROUP, (group + 1) * GROUP)
        pieces = [inner_t[chans, i * KMR : (i + 2) * KMR] for i in range(spans)]
        out = jnp.dot(
            jnp.concatenate(pieces, axis=0), band_ref[group], preferred_element_type=jnp.float32
        )
        for i in range(spans):
            mixed_t[chans, i * KMR : (i + 1) * KMR] = out[i * GROUP : (i + 1) * GROUP]
    for i in range(spans):
        query = short_rows(q_ext, taps_q, block + i * KMR, KMR).T
        mixed = mixed_t[:, i * KMR : (i + 1) * KMR]
        gated_ref[:, i * KMR : (i + 1) * KMR] = (query * mixed).astype(gated_ref.dtype)


def project_kernel(place_ref, own_ref, pair_ref, weight_ref, out_ref, both):
    @pl.when(pl.program_id(0) == 0)
    def _():
        slot = place_ref[0]
        both[slot] = own_ref[...]
        both[1 - slot] = pair_ref[...]

    steps, cores, _, yl_size, _, _ = weight_ref.shape
    for step in range(steps):
        total = None
        for slot in range(2):
            pieces = [weight_ref[step, core, slot, yl] for yl in range(yl_size) for core in range(cores)]
            term = jnp.dot(
                jnp.concatenate(pieces, axis=0), both[slot], preferred_element_type=jnp.float32
            )
            total = term if total is None else total + term
        out_ref[step] = total.astype(out_ref.dtype)


def prefetch_kernel(weight_ref, out_ref, arrived):
    copies = [
        pltpu.make_async_copy(weight_ref.at[i], out_ref.at[i], arrived.at[i])
        for i in range(out_ref.shape[0])
    ]
    for copy in copies:
        copy.start()
    for copy in copies:
        copy.wait()


def sum_kernel(place_ref, parts_ref, residual_ref, out_ref):
    total = parts_ref[0].astype(jnp.float32)
    for i in range(1, parts_ref.shape[0]):
        total = total + parts_ref[i].astype(jnp.float32)
    half = total.shape[0] // 2
    first, second = total[:half], total[half:]
    for i, (piece, swapped) in enumerate(((first, second), (second, first))):
        lanes = slice(i * half, (i + 1) * half)
        piece = jnp.where(place_ref[0] == 0, piece, swapped).T
        out_ref[:, lanes] = (residual_ref[:, lanes].astype(jnp.float32) + piece).astype(out_ref.dtype)


def weight_route(pair_step, yl_step):
    return [
        ((yh * 2 + yl) * 2 + par, ((par ^ pair_step) * 2 + (yl ^ yl_step)) * 2 + yh)
        for yh in range(2)
        for yl in range(2)
        for par in range(2)
    ]


def body(features, short_taps, mr_filter, out_weight, residual):
    block, _, width = features.shape
    sources = lax.axis_size(CHAN)
    chans = width // sources
    tokens = sources * block
    bf16, f32 = jnp.bfloat16, jnp.float32
    vmem = pl.BlockSpec(memory_space=pltpu.VMEM)
    smem = pl.BlockSpec(memory_space=pltpu.SMEM)

    near = []
    for pair_step in range(2):
        for yl_step in range(2):
            near.append(
                lax.ppermute(out_weight.T, ("yh", "yl", "par"), weight_route(pair_step, yl_step))
            )
    cols = near[0].shape[0]
    near = jnp.stack(near).reshape(2, 2, cols, chans)
    whole_weight = lax.all_gather(near, ("x", "core"), axis=0)
    x_size = lax.axis_size("x")
    whole_weight = whole_weight.reshape(x_size, -1, *near.shape)

    sent = features.reshape(block, 3, sources, chans).transpose(2, 1, 0, 3)
    rows = lax.all_to_all(sent, CHAN, 0, 0, tiled=True)
    halo_blocks = -(-(KMR + KS - 1) // block)
    tail = jnp.concatenate(
        [rows[sources - halo_blocks :, 1:].reshape(2 * halo_blocks, block, chans), rows[sources - 1 :, 0]],
        axis=0,
    )
    shards = lax.axis_size(SEQ)
    halo = lax.ppermute(tail, SEQ, [(i, i + 1) for i in range(shards - 1)])

    groups = mr_filter.shape[0]
    band = call(
        bands_kernel,
        flops=groups * KMR * KMR * 4,
        moved=groups * 2 * KMR * KMR * 2,
        out_shape=jax.ShapeDtypeStruct((groups, 2 * KMR, KMR), bf16),
        in_specs=[vmem],
        out_specs=vmem,
    )(mr_filter)

    per_step = LANES // GROUP
    halo_rows = halo_blocks * block
    gated = call(
        conv_kernel,
        flops=tokens * chans * 256 * 2,
        moved=rows.size * 2 + halo.size * 2 + band.size * 2,
        grid=(chans // LANES,),
        out_shape=jax.ShapeDtypeStruct((chans, tokens), bf16),
        in_specs=[
            pl.BlockSpec((sources, 3, block, LANES), lambda i: (0, 0, 0, i)),
            pl.BlockSpec((2 * halo_blocks + 1, block, LANES), lambda i: (0, 0, i)),
            pl.BlockSpec((3, KS, LANES), lambda i: (0, 0, i)),
            pl.BlockSpec((per_step, 2 * KMR, KMR), lambda i: (i, 0, 0)),
        ],
        out_specs=pl.BlockSpec((LANES, tokens), lambda i: (i, 0)),
        scratch_shapes=[
            pltpu.VMEM((block + tokens, LANES), f32),
            pltpu.VMEM((halo_rows + tokens, LANES), f32),
            pltpu.VMEM((halo_rows + tokens, LANES), f32),
            pltpu.VMEM((LANES, KMR + tokens), bf16),
            pltpu.VMEM((LANES, tokens), f32),
        ],
    )(rows, halo, short_taps.transpose(1, 0, 2), band)

    pair = lax.ppermute(gated, "par", [(0, 1), (1, 0)])
    whole_weight, gated = lax.optimization_barrier((whole_weight, gated))
    whole_weight = pltpu.with_memory_space_constraint(whole_weight, pltpu.HBM)
    whole_weight = call(
        prefetch_kernel,
        vmem_mib=20,
        moved=whole_weight.size * 4,
        out_shape=jax.ShapeDtypeStruct(whole_weight.shape, bf16),
        in_specs=[pl.BlockSpec(memory_space=pltpu.HBM)],
        out_specs=vmem,
        scratch_shapes=[pltpu.SemaphoreType.DMA((x_size,))],
    )(whole_weight)
    out_cols = whole_weight.size // (x_size * 2 * chans)
    both = pl.BlockSpec((chans, tokens), lambda i: (0, 0))
    per_call = 2
    partial = call(
        project_kernel,
        vmem_mib=20,
        flops=tokens * 2 * chans * x_size * out_cols * 2,
        moved=whole_weight.size * 2 + x_size * tokens * out_cols * 2 + gated.size * 4,
        grid=(x_size // per_call,),
        out_shape=jax.ShapeDtypeStruct((x_size, out_cols, tokens), bf16),
        in_specs=[
            smem,
            both,
            both,
            pl.BlockSpec((per_call, *whole_weight.shape[1:]), lambda i: (i, 0, 0, 0, 0, 0)),
        ],
        out_specs=pl.BlockSpec((per_call, out_cols, tokens), lambda i: (i, 0, 0)),
        scratch_shapes=[pltpu.VMEM((2, chans, tokens), bf16)],
    )((lax.axis_index("par") ^ lax.axis_index("yh")).reshape(1), gated, pair, whole_weight)

    parts = lax.all_to_all(partial, ("Y", "zz"), 0, 0, tiled=True)
    return call(
        sum_kernel,
        flops=parts.size,
        moved=parts.size * 2 + residual.size * 4,
        out_shape=jax.ShapeDtypeStruct(residual.shape, residual.dtype),
        in_specs=[smem, vmem, vmem],
        out_specs=vmem,
    )(lax.axis_index("yl").reshape(1), parts, residual)


def split(mesh, sizes):
    return Mesh(mesh.devices.reshape(sizes), SEQ + CHAN)


def solution(mesh):
    fine = split(mesh, (8, 2, 2, 2, 2, 4, 2))
    placed = (
        P(SEQ + CHAN, None, None),
        P(None, None, CHAN),
        P(CHAN, None),
        P(CHAN, SEQ),
        P(SEQ, CHAN),
    )
    return jax.shard_map(body, mesh=fine, in_specs=placed, out_specs=P(SEQ, CHAN), check_vma=False)
```
